128 devices in a mesh: bond: 8 (over y, core), atom: 16 (over z, x).
Axes of the slice: x: 4, y: 4, z: 4, core: 2. Of those that a mesh axis runs over, the one named last changes fastest.
Arguments:
- bond_states: bfloat16 [262144, 512], P(('bond', 'atom')), may hold values from -6 to 6
- block_counts: int32 [128], P(('bond', 'atom')), may hold values from 8 to 64, as said below
- send_rows: int32 [128, 128, 64], P(('bond', 'atom')), may hold values from 0 to 2047
- source_slots: int32 [128, 2048], P(('bond', 'atom')), may hold values from 0 to 8191
- target_slots: int32 [128, 2048], P(('bond', 'atom')), may hold values from 0 to 4095
- return_rows: int32 [128, 4096], P(('bond', 'atom')), may hold values from 0 to 2047
- angular_basis: bfloat16 [8192, 32, 512], P(('bond', 'atom')), may hold values from -1 to 1
- pre_inner: bfloat16 [2, 512, 512], replicated, may hold values from -0.25 to 0.25
- pre_outer: bfloat16 [2, 512, 512], replicated, may hold values from -0.25 to 0.25
- down_proj: bfloat16 [2, 512, 64], replicated, may hold values from -0.25 to 0.25
- bilinear: bfloat16 [2, 1024, 64], replicated, may hold values from -0.1875 to 0.1875
- up_proj: bfloat16 [2, 64, 512], replicated, may hold values from -0.75 to 0.75
- post_inner: bfloat16 [2, 512, 512], replicated, may hold values from -0.25 to 0.25
- post_outer: bfloat16 [2, 512, 512], replicated, may hold values from -0.25 to 0.25
Outputs:
- bond_out: bfloat16 [262144, 512], P(('bond', 'atom'))
The draws below stay inside these ranges and needn't reach their ends.
Inputs may be any that keep to these rules, and one draw needn't show every extreme that they name: Owner o's blocks numbered below block_counts[o] are live, the others are padding; some owner has all 64 live in every draw.
All inputs are finite; a program needn't handle non-finite values.
Results may differ from the reference program's by a relative error of at most 0.0078.
Values may be sent and summed in bfloat16 or wider, within the bound.
A program may use at most 128 MiB of HBM per device.

```python
import jax
import jax.numpy as jnp
from jax import lax

D = 512
TRIP = 64
NSPH = 16
BLK = 32
LAYERS = 2
CAP = 64
CAP2 = 32
BOND_DEV = 2048
NB = 64
PEERS = 128
BONDS = 262144


def draw_block_counts(key, part):
    first_key = jax.random.fold_in(key, 11)
    second_key = jax.random.fold_in(key, 12)
    lowest = max(1, NB // 8)
    counts = jax.random.randint(first_key, (PEERS,), lowest, NB // 2 + 1, dtype=jnp.int32)
    busiest = jax.random.randint(second_key, (4,), 0, PEERS, dtype=jnp.int32)
    counts = counts.at[busiest].set(NB)
    return counts.astype(jnp.int32)


def plant(result, rng, low, largest):
    spot = [jax.random.randint(jax.random.fold_in(rng, axis), (), 0, length) for axis, length in enumerate(result.shape)]
    main_axis = result.shape.index(max(result.shape))
    beside = spot[:main_axis] + [(spot[main_axis] + 1) % result.shape[main_axis]] + spot[main_axis + 1:]
    return result.at[tuple(spot)].set(low).at[tuple(beside)].set(largest)


def shard_levels(rng, extent, cuts, low, top_value):
    def one(dim, blocks):
        heights = jax.random.uniform(jax.random.fold_in(jax.random.fold_in(rng, 6), dim), (blocks,), jnp.float32, low / len(cuts), top_value / len(cuts))
        return jnp.repeat(jnp.exp(heights), extent[dim] // blocks).reshape((-1,) + (1,) * (len(extent) - dim - 1))

    level = one(*cuts[0])
    for cut in cuts[1:]:
        level = level * one(*cut)
    return level


def normal_values(rng, extent, width, bound, cuts=(), held_as=jnp.bfloat16):
    gain = shard_levels(rng, extent, cuts, -0.22, 0.18) if cuts else 1.0
    array = jax.random.normal(rng, extent, jnp.float32) * width * gain
    return jnp.minimum(jnp.maximum(array, -bound), bound).astype(held_as)


def setup_inputs(seed: int = 0) -> dict:
    seeds = jax.random.split(jax.random.key(seed), 15)
    bond_states = normal_values(seeds[0], (BONDS, D), 1.0, 6.0, ((0, 128),))
    block_counts = draw_block_counts(jax.random.fold_in(seeds[14], 71), 0)
    send_rows = plant(jax.random.randint(seeds[2], (PEERS, PEERS, CAP), 0, BOND_DEV), jax.random.fold_in(seeds[2], 1), 0, BOND_DEV - 1).astype(jnp.int32)
    source_slots = plant(jax.random.randint(seeds[3], (PEERS, NB * BLK), 0, PEERS * CAP), jax.random.fold_in(seeds[3], 1), 0, (PEERS * CAP) - 1).astype(jnp.int32)
    target_slots = plant(jax.random.randint(seeds[4], (PEERS, NB * BLK), 0, PEERS * CAP2), jax.random.fold_in(seeds[4], 1), 0, (PEERS * CAP2) - 1).astype(jnp.int32)
    return_rows = plant(jax.random.randint(seeds[5], (PEERS, PEERS * CAP2), 0, BOND_DEV), jax.random.fold_in(seeds[5], 1), 0, BOND_DEV - 1).astype(jnp.int32)
    angular_basis = normal_values(seeds[6], (PEERS * NB, BLK, BLK * NSPH), BLK ** -0.5, 1.0, ((0, 128),))
    pre_inner = normal_values(seeds[7], (LAYERS, D, D), D ** -0.5, 0.25)
    pre_outer = normal_values(seeds[8], (LAYERS, D, D), D ** -0.5, 0.25)
    down_proj = normal_values(seeds[9], (LAYERS, D, TRIP), D ** -0.5, 0.25)
    bilinear = normal_values(seeds[10], (LAYERS, NSPH * TRIP, TRIP), (NSPH * TRIP) ** -0.5, 0.1875)
    up_proj = normal_values(seeds[11], (LAYERS, TRIP, D), TRIP ** -0.5, 0.75)
    post_inner = normal_values(seeds[12], (LAYERS, D, D), D ** -0.5, 0.25)
    post_outer = normal_values(seeds[13], (LAYERS, D, D), D ** -0.5, 0.25)
    return dict(bond_states=bond_states, block_counts=block_counts, send_rows=send_rows, source_slots=source_slots, target_slots=target_slots, return_rows=return_rows, angular_basis=angular_basis, pre_inner=pre_inner, pre_outer=pre_outer, down_proj=down_proj, bilinear=bilinear, up_proj=up_proj, post_inner=post_inner, post_outer=post_outer)


root_half = 0.7071067811865476


def residual(states, inner_weight, outer_weight):
    hidden = jax.nn.silu(jnp.dot(states, inner_weight, preferred_element_type=jnp.float32)).astype(jnp.bfloat16)
    return (states.astype(jnp.float32) + jax.nn.silu(jnp.dot(hidden, outer_weight, preferred_element_type=jnp.float32))) * root_half


def reference(bond_states, block_counts, send_rows, source_slots, target_slots, return_rows, angular_basis, pre_inner, pre_outer, down_proj, bilinear, up_proj, post_inner, post_outer):
    device_ids = jnp.arange(PEERS, dtype=jnp.int32)
    fetch_rows = (send_rows + device_ids[:, None, None] * BOND_DEV).astype(jnp.int32)
    fetch_rows = jnp.transpose(fetch_rows, (1, 0, 2)).reshape(PEERS, PEERS * CAP)
    block_basis = angular_basis.reshape(PEERS, NB, BLK, BLK * NSPH)
    live_blocks = (jnp.arange(NB, dtype=jnp.int32)[None, :] < block_counts[:, None]).astype(jnp.float32)
    return_ids = (return_rows + device_ids[:, None] * BOND_DEV).astype(jnp.int32).reshape(-1)
    states = bond_states
    for layer_index in range(LAYERS):
        inner_state = residual(states, pre_inner[layer_index], pre_outer[layer_index]).astype(jnp.bfloat16)
        projected = jax.nn.silu(jnp.dot(inner_state, down_proj[layer_index], preferred_element_type=jnp.float32)).astype(jnp.bfloat16)
        weight_bil = bilinear[layer_index]

        def owner_work(pieces):
            fetch_owner, source_owner, target_owner, basis_owner, live_owner = pieces
            provided = projected[fetch_owner]
            gathered = provided[source_owner].reshape(NB, BLK, TRIP)
            contracted = jnp.einsum("bsx,bsc->bxc", basis_owner.astype(jnp.float32), gathered.astype(jnp.float32)).astype(jnp.bfloat16)
            partial_rows = jnp.dot(contracted.reshape(NB * BLK, NSPH * TRIP), weight_bil, preferred_element_type=jnp.float32)
            partial_rows = partial_rows * jnp.repeat(live_owner, BLK)[:, None]
            slot_sums = jax.ops.segment_sum(partial_rows, target_owner, num_segments=PEERS * CAP2)
            return slot_sums.astype(jnp.bfloat16)

        slot_sums = lax.map(owner_work, (fetch_rows, source_slots, target_slots, block_basis, live_blocks))
        values = jnp.transpose(slot_sums.reshape(PEERS, PEERS, CAP2, TRIP), (1, 0, 2, 3)).reshape(-1, TRIP)
        message = jax.ops.segment_sum(values.astype(jnp.float32), return_ids, num_segments=BONDS).astype(jnp.bfloat16)
        joined = ((inner_state.astype(jnp.float32) + jax.nn.silu(jnp.dot(message, up_proj[layer_index], preferred_element_type=jnp.float32))) * root_half).astype(jnp.bfloat16)
        states = residual(joined, post_inner[layer_index], post_outer[layer_index]).astype(jnp.bfloat16)
    return states
```

```python
import functools

import jax
import jax.numpy as jnp
from jax import lax
from jax.experimental import pallas as pl
from jax.experimental.pallas import tpu as pltpu
from jax.sharding import PartitionSpec as P

MESH = pl.DeviceIdType.MESH
root_half = 0.7071067811865476
bf16 = jnp.bfloat16
f32 = jnp.float32
i32 = jnp.int32


def dot(a, b):
    return jnp.dot(a, b, preferred_element_type=f32)


def silu(v):
    half = 0.5 * v
    return half * jnp.tanh(half) + half


def lanes(shape):
    return lax.broadcasted_iota(i32, shape, 1)


def one_hot(index, positions):
    return jnp.where(index == positions, 1.0, 0.0).astype(bf16)


def kernel(
    count_ref,
    x_ref,
    send_ref,
    source_ref,
    target_ref,
    target_row_ref,
    return_ref,
    return_row_ref,
    basis_ref,
    pre_in_ref,
    pre_out_ref,
    down_ref,
    bil_ref,
    up_ref,
    post_in_ref,
    post_out_ref,
    out_ref,
    inner,
    down_wide,
    up_tall,
    table,
    pick_send,
    col_send,
    pick_source,
    col_source,
    pick_target,
    col_target,
    pick_return,
    col_return,
    basis_t,
    turned,
    bil_wide,
    payload,
    arrived,
    gathered,
    mixed,
    partial,
    spread,
    outgoing,
    incoming,
    spread_in,
    message,
    send_sem,
    recv_sem,
):
    me_bond = lax.axis_index("bond")
    me_atom = lax.axis_index("atom")
    atoms = 16
    peers = 128
    me = me_bond * atoms + me_atom
    layers = 2

    barrier = pltpu.get_barrier_semaphore()

    def greet(step, carry):
        peer = lax.rem(me + step, peers)
        pl.semaphore_signal(
            barrier, inc=1, device_id=(peer // atoms, lax.rem(peer, atoms)), device_id_type=MESH
        )
        return carry

    lax.fori_loop(1, peers, greet, 0)

    lane128 = lanes((1, 128))
    low_half = lane128 < 64
    half_id = lane128 // 64
    lane256 = lanes((1, 256))
    group_id = lane256 // 64

    send_t = jnp.transpose(send_ref[...])
    for c in range(16):
        col_send[c] = send_t[:, c * 8 : (c + 1) * 8]

    def build_send(c, carry):
        cols = col_send[c]
        pos = lanes((32, 512))
        for h in range(2):
            for o in range(8):
                col = cols[h * 32 : (h + 1) * 32, o : o + 1]
                pick_send[c, h * 256 + o * 32 : h * 256 + (o + 1) * 32, :] = one_hot(col & 511, pos)
        return carry

    lax.fori_loop(0, 16, build_send, 0)

    for l in range(layers):
        for g in range(4):
            down_wide[l, :, g * 64 : (g + 1) * 64] = down_ref[l]
            up_tall[l, g * 64 : (g + 1) * 64, :] = up_ref[l]

    def residual(v, w_in, w_out):
        hidden = silu(dot(v, w_in)).astype(bf16)
        return ((v.astype(f32) + silu(dot(hidden, w_out))) * root_half).astype(bf16)

    def pre(l, g, v):
        inner_g = residual(v, pre_in_ref[l], pre_out_ref[l])
        inner[pl.ds(g * 512, 512), :] = inner_g
        proj = silu(dot(inner_g, down_wide[l])).astype(bf16)
        table[...] = jnp.where(group_id == g, proj, table[...])

    def first(g, carry):
        pre(0, g, x_ref[pl.ds(g * 512, 512), :])
        return carry

    table[...] = jnp.zeros_like(table)
    lax.fori_loop(0, 4, first, 0)

    pl.semaphore_wait(barrier, peers - 1)

    def send_block(src, dst, peer, sem_index, recv):
        @pl.when(peer != me)
        def _():
            pltpu.make_async_remote_copy(
                src_ref=src,
                dst_ref=dst,
                send_sem=send_sem.at[sem_index],
                recv_sem=recv,
                device_id=(peer // atoms, lax.rem(peer, atoms)),
                device_id_type=MESH,
            ).start()

        @pl.when(peer == me)
        def _():
            pltpu.make_async_copy(src, dst, recv).start()

    def provide(l):
        def send_chunk(c):
            for o in range(8):
                peer = c * 8 + o
                send_block(
                    payload.at[peer],
                    arrived.at[l, me // 2, lax.rem(me, 2)],
                    peer,
                    l * 2,
                    recv_sem.at[l * 8 + me // 32],
                )

        def chunk(step, carry):
            c = lax.rem(me // 8 + step, 16)
            values = dot(pick_send[c], table[...])
            cols = col_send[c]
            for o in range(8):
                half = []
                for h in range(2):
                    low = cols[h * 32 : (h + 1) * 32, o : o + 1] >> 9
                    e = values[h * 256 + o * 32 : h * 256 + (o + 1) * 32]
                    v = jnp.where(low >= 2, e[:, 128:], e[:, :128])
                    half.append((v, pltpu.roll(v, 64, 1), (low & 1) == 1))
                (v0, w0, odd0), (v1, w1, odd1) = half
                picked = jnp.where(low_half, jnp.where(odd0, w0, v0), jnp.where(odd1, v1, w1))
                payload[c * 8 + o] = picked.astype(bf16)

            @pl.when(step > 0)
            def _():
                send_chunk(lax.rem(me // 8 + step + 15, 16))

            return carry

        lax.fori_loop(0, 16, chunk, 0)
        send_chunk(lax.rem(me // 8 + 15, 16))

    def prepare():
        source_t = jnp.transpose(source_ref[...])
        target_t = jnp.transpose(target_ref[...])
        return_t = jnp.transpose(return_ref[...])
        rows = lax.broadcasted_iota(i32, (128, 1), 0) // 32
        for c in range(16):
            col_source[c] = source_t[:, c : c + 1]
            t = target_t[:, c : c + 1]
            low = ((t >> 5) & 1) * 2 + ((t >> 4) & 1)
            col_target[c] = jnp.where(rows + c * 4 < count_ref[0], low, -1)
        for c in range(32):
            col_return[c] = return_t[:, c : c + 1] >> 9

        def build_source(c, carry):
            s = col_source[c]
            key = (s >> 7) * 32 + (s & 31)
            for k in range(4):
                pick_source[k, pl.ds(c * 128, 128), :] = one_hot(key, lanes((128, 512)) + k * 512)
            return carry

        lax.fori_loop(0, 16, build_source, 0)

        t = target_row_ref[...]
        target_key = (t >> 6) * 16 + (t & 15)

        def build_target(c, carry):
            pos = lax.broadcasted_iota(i32, (64, 2048), 0) + c * 64
            pick_target[pl.ds(c * 64, 64), :] = one_hot(target_key, pos)
            return carry

        lax.fori_loop(0, 16, build_target, 0)

        return_key = return_row_ref[...] & 511

        def build_return(c, carry):
            pos = lax.broadcasted_iota(i32, (64, 1024), 0) + c * 64
            for k in range(4):
                key = return_key[:, k * 1024 : (k + 1) * 1024]
                pick_return[k, pl.ds(c * 64, 64), :] = one_hot(key, pos)
            return carry

        lax.fori_loop(0, 8, build_return, 0)

        def turn(g, carry):
            block = basis_ref[pl.ds(g * 4, 4)].reshape(128, 512).astype(f32)
            turned[...] = jnp.transpose(block)
            for k in range(16):
                basis_t[g, k * 32 : (k + 1) * 32, :] = turned[pl.ds(k, 32, stride=16), :].astype(bf16)
            return carry

        lax.fori_loop(0, 16, turn, 0)

        bil_wide[...] = jnp.zeros_like(bil_wide)
        for l in range(layers):

            def widen(k, carry):
                w = bil_ref[l, pl.ds(k * 64, 64), :]
                for b in range(4):
                    bil_wide[l, pl.ds(k * 256 + b * 64, 64), b * 64 : (b + 1) * 64] = w
                return carry

            lax.fori_loop(0, 16, widen, 0)

    def triplet(l):
        for n in range(4):
            k = lax.rem(me // 32 + 4 - n, 4)
            pltpu.make_async_copy(
                arrived.at[l, pl.ds(0, 16)], arrived.at[l, pl.ds(0, 16)], recv_sem.at[l * 8 + k]
            ).wait()
            block = jnp.concatenate(
                [
                    arrived[l, pl.ds(k * 16, 16), 0].reshape(512, 128),
                    arrived[l, pl.ds(k * 16, 16), 1].reshape(512, 128),
                ],
                axis=1,
            )

            def gather(m, carry):
                part = dot(pick_source[k, pl.ds(m * 512, 512), :], block)
                if n > 0:
                    part = part + gathered[pl.ds(m * 512, 512), :]
                gathered[pl.ds(m * 512, 512), :] = part
                return carry

            lax.fori_loop(0, 4, gather, 0)

        row_block = lax.broadcasted_iota(i32, (128, 1), 0) // 32

        def contract(g, carry):
            s = col_source[g]
            a = gathered[pl.ds(g * 128, 128), :]
            v = jnp.where(((s >> 6) & 1) == 1, a[:, 128:], a[:, :128])
            w = pltpu.roll(v, 64, 1)
            both = jnp.where(((s >> 5) & 1) != half_id, w, v)
            right = jnp.concatenate(
                [
                    jnp.where(row_block == half_id, both, 0.0),
                    jnp.where(row_block == half_id + 2, both, 0.0),
                ],
                axis=1,
            ).astype(bf16)
            c = dot(basis_t[g], right).astype(bf16)
            for k in range(16):
                mixed[pl.ds(g * 32, 32), k * 256 : (k + 1) * 256] = c[k * 32 : (k + 1) * 32]
            return carry

        lax.fori_loop(0, 16, contract, 0)

        partial[...] = dot(mixed[...], bil_wide[l])

        def scatter(g, carry):
            p = partial[pl.ds(g * 32, 32), :]
            for half in range(2):
                v = p[:, half * 128 : (half + 1) * 128]
                w = pltpu.roll(v, 64, 1)
                for b in range(2):
                    both = jnp.where(low_half, v, w) if b == 0 else jnp.where(low_half, w, v)
                    b4 = half * 2 + b
                    low = col_target[g, b4 * 32 : (b4 + 1) * 32, :]
                    rows = pl.ds(g * 128 + b4 * 32, 32)
                    spread[rows, 0:128] = jnp.where(low == half_id, both, 0.0).astype(bf16)
                    spread[rows, 128:256] = jnp.where(low == half_id + 2, both, 0.0).astype(bf16)
            return carry

        lax.fori_loop(0, 16, scatter, 0)

    def give_back(l):
        def send_chunk(c):
            def one(i, carry):
                peer = c * 32 + i
                send_block(
                    outgoing.at[peer // 2, lax.rem(peer, 2)],
                    incoming.at[l, me],
                    peer,
                    l * 2 + 1,
                    recv_sem.at[l * 8 + 4 + me // 32],
                )
                return carry

            lax.fori_loop(0, 32, one, 0)

        def chunk(n, carry):
            c = lax.rem(me // 32 + n, 4)
            sums = dot(pick_target[pl.ds(c * 256, 256), :], spread[...]).astype(bf16)
            outgoing[pl.ds(c * 16, 16), 0] = sums[:, :128].reshape(16, 16, 128)
            outgoing[pl.ds(c * 16, 16), 1] = sums[:, 128:].reshape(16, 16, 128)

            @pl.when(n > 0)
            def _():
                send_chunk(lax.rem(me // 32 + n + 3, 4))

            return carry

        lax.fori_loop(0, 4, chunk, 0)
        send_chunk(lax.rem(me // 32 + 3, 4))

    def receive(l):
        for n in range(4):
            c = lax.rem(me // 32 + 4 - n, 4)
            pltpu.make_async_copy(
                incoming.at[l, pl.ds(0, 32)], incoming.at[l, pl.ds(0, 32)], recv_sem.at[l * 8 + 4 + c]
            ).wait()

            def place(q, carry):
                for o in range(4):
                    v = incoming[l, c * 32 + q * 4 + o].astype(f32)
                    w = pltpu.roll(v, 64, 1)
                    for h in range(2):
                        both = jnp.where(low_half, v, w) if h == 0 else jnp.where(low_half, w, v)
                        low = col_return[c * 8 + q, o * 32 + h * 16 : o * 32 + (h + 1) * 16, :]
                        rows = pl.ds(q * 128 + o * 32 + h * 16, 16)
                        spread_in[rows, 0:128] = jnp.where(low == half_id, both, 0.0).astype(bf16)
                        spread_in[rows, 128:256] = jnp.where(low == half_id + 2, both, 0.0).astype(bf16)
                return carry

            lax.fori_loop(0, 8, place, 0)
            part = dot(pick_return[c], spread_in[...])
            if n > 0:
                part = part + message[...]
            message[...] = part

    def post(l, g):
        picked = jnp.where(group_id == g, message[...], 0.0).astype(bf16)
        added = silu(dot(picked, up_tall[l]))
        joined = ((inner[pl.ds(g * 512, 512), :].astype(f32) + added) * root_half).astype(bf16)
        return residual(joined, post_in_ref[l], post_out_ref[l])

    def sent(rows, index):
        pltpu.make_async_copy(rows, rows, send_sem.at[index]).wait()

    for l in range(layers):
        provide(l)
        if l == 0:
            prepare()
        triplet(l)
        sent(payload.at[pl.ds(0, peers - 1)], l * 2)
        give_back(l)
        receive(l)
        sent(incoming.at[l, pl.ds(0, peers - 1)], l * 2 + 1)
        if l < layers - 1:

            def middle(g, carry):
                pre(l + 1, g, post(l, g))
                return carry

            lax.fori_loop(0, 4, middle, 0)
        else:

            def last(g, carry):
                out_ref[pl.ds(g * 512, 512), :] = post(l, g)
                return carry

            lax.fori_loop(0, 4, last, 0)


def on_device(
    bond_states,
    block_counts,
    send_rows,
    source_slots,
    target_slots,
    return_rows,
    angular_basis,
    pre_inner,
    pre_outer,
    down_proj,
    bilinear,
    up_proj,
    post_inner,
    post_outer,
):
    vmem = pl.BlockSpec(memory_space=pltpu.VMEM)
    return pl.pallas_call(
        kernel,
        name="triplet",
        out_shape=jax.ShapeDtypeStruct((2048, 512), bf16),
        in_specs=[pl.BlockSpec(memory_space=pltpu.SMEM)] + [vmem] * 15,
        out_specs=vmem,
        scratch_shapes=[
            pltpu.VMEM((2048, 512), bf16),
            pltpu.VMEM((2, 512, 256), bf16),
            pltpu.VMEM((2, 256, 512), bf16),
            pltpu.VMEM((512, 256), bf16),
            pltpu.VMEM((16, 512, 512), bf16),
            pltpu.VMEM((16, 64, 8), i32),
            pltpu.VMEM((4, 2048, 512), bf16),
            pltpu.VMEM((16, 128, 1), i32),
            pltpu.VMEM((1024, 2048), bf16),
            pltpu.VMEM((16, 128, 1), i32),
            pltpu.VMEM((4, 512, 1024), bf16),
            pltpu.VMEM((32, 128, 1), i32),
            pltpu.VMEM((16, 512, 128), bf16),
            pltpu.VMEM((512, 128), f32),
            pltpu.VMEM((2, 4096, 256), bf16),
            pltpu.VMEM((128, 32, 128), bf16),
            pltpu.VMEM((2, 64, 2, 32, 128), bf16),
            pltpu.VMEM((2048, 256), f32),
            pltpu.VMEM((512, 4096), bf16),
            pltpu.VMEM((512, 256), f32),
            pltpu.VMEM((2048, 256), bf16),
            pltpu.VMEM((64, 2, 16, 128), bf16),
            pltpu.VMEM((2, 128, 16, 128), bf16),
            pltpu.VMEM((1024, 256), bf16),
            pltpu.VMEM((512, 256), f32),
            pltpu.SemaphoreType.DMA((4,)),
            pltpu.SemaphoreType.DMA((16,)),
        ],
        compiler_params=pltpu.CompilerParams(
            collective_id=0, has_side_effects=True, vmem_limit_bytes=67043328
        ),
    )(
        block_counts,
        bond_states,
        send_rows[0],
        source_slots.reshape(16, 128),
        target_slots.reshape(16, 128),
        target_slots,
        return_rows.reshape(32, 128),
        return_rows,
        angular_basis,
        pre_inner,
        pre_outer,
        down_proj,
        bilinear,
        up_proj,
        post_inner,
        post_outer,
    )


def solution(mesh):
    split = ("bond", "atom")
    in_specs = (
        P(split, None),
        P(split),
        P(split, None, None),
        P(split, None),
        P(split, None),
        P(split, None),
        P(split, None, None),
    ) + (P(),) * 7
    return jax.shard_map(
        on_device, mesh=mesh, in_specs=in_specs, out_specs=P(split, None), check_vma=False
    )
```

```python
import functools

import jax
import jax.numpy as jnp
from jax import lax
from jax.experimental import pallas as pl
from jax.experimental.pallas import tpu as pltpu
from jax.sharding import PartitionSpec as P

MESH = pl.DeviceIdType.MESH
root_half = 0.7071067811865476
bf16 = jnp.bfloat16
f32 = jnp.float32
i32 = jnp.int32


def dot(a, b):
    return jnp.dot(a, b, preferred_element_type=f32)


def silu(v):
    half = 0.5 * v
    return half * jnp.tanh(half) + half


def lanes(shape):
    return lax.broadcasted_iota(i32, shape, 1)


def one_hot(index, positions):
    return jnp.where(index == positions, 1.0, 0.0).astype(bf16)


def loop(count, unroll, body):
    def some(step, carry):
        for u in range(unroll):
            body(step * unroll + u)
        return carry

    if count == unroll:
        some(0, 0)
    else:
        lax.fori_loop(0, count // unroll, some, 0)


def residual(v, w_in, w_out):
    hidden = silu(dot(v, w_in)).astype(bf16)
    return ((v.astype(f32) + silu(dot(hidden, w_out))) * root_half).astype(bf16)


def join(g, inner_g, message, up_tall):
    group_id = lanes((1, 256)) // 64
    picked = jnp.where(group_id == g, message, jnp.zeros_like(message))
    added = silu(dot(picked, up_tall))
    return ((inner_g.astype(f32) + added) * root_half).astype(bf16)


def final(inner_ref, message_ref, up_ref, w_in_ref, w_out_ref, out_ref):
    up_tall = jnp.concatenate([up_ref[0]] * 4, axis=0)
    joined = join(pl.program_id(0), inner_ref[...], message_ref[...], up_tall)
    out_ref[...] = residual(joined, w_in_ref[0], w_out_ref[0])


def kernel(
    count_ref,
    send_ref,
    source_ref,
    target_ref,
    target_row_ref,
    return_ref,
    return_row_ref,
    x_hbm,
    basis_hbm,
    pre_in_hbm,
    pre_out_hbm,
    down_hbm,
    bil_hbm,
    up_hbm,
    post_in_hbm,
    post_out_hbm,
    inner_hbm,
    message_ref,
    basis_ref,
    pre_in_ref,
    pre_out_ref,
    down_ref,
    bil_ref,
    up_ref,
    post_in_ref,
    post_out_ref,
    inner,
    down_wide,
    up_tall,
    table,
    pick_send,
    col_send,
    pick_source,
    col_source,
    pick_target,
    col_target,
    pick_return,
    col_return,
    basis_t,
    turned,
    bil_wide,
    payload,
    arrived,
    gathered,
    mixed,
    partial,
    spread,
    outgoing,
    incoming,
    spread_in,
    message,
    send_sem,
    recv_sem,
    load_sem,
):
    me_bond = lax.axis_index("bond")
    me_atom = lax.axis_index("atom")
    atoms = 16
    peers = 128
    me = me_bond * atoms + me_atom
    layers = 2

    barrier = pltpu.get_barrier_semaphore()

    def greet(step, carry):
        peer = lax.rem(me + step, peers)
        pl.semaphore_signal(
            barrier, inc=1, device_id=(peer // atoms, lax.rem(peer, atoms)), device_id_type=MESH
        )
        return carry

    lax.fori_loop(1, peers, greet, 0)

    loads = [
        pltpu.make_async_copy(src, dst, load_sem.at[n])
        for n, (src, dst) in enumerate(
            (
                (down_hbm, down_ref),
                (pre_in_hbm, pre_in_ref),
                (pre_out_hbm, pre_out_ref),
                (x_hbm, inner),
                (basis_hbm, basis_ref),
                (bil_hbm, bil_ref),
                (up_hbm, up_ref),
                (post_in_hbm.at[0], post_in_ref),
                (post_out_hbm.at[0], post_out_ref),
            )
        )
    ]
    for copy in loads:
        copy.start()
    store = pltpu.make_async_copy(inner, inner_hbm, load_sem.at[len(loads)])

    lane128 = lanes((1, 128))
    low_half = lane128 < 64
    half_id = lane128 // 64
    lane256 = lanes((1, 256))
    group_id = lane256 // 64

    for c in range(16):
        col_send[c] = send_ref[:, c * 8 : (c + 1) * 8]

    def build_send(c):
        cols = col_send[c]
        pos = lanes((32, 512))
        for h in range(2):
            for o in range(8):
                col = cols[h * 32 : (h + 1) * 32, o : o + 1]
                pick_send[c, h * 256 + o * 32 : h * 256 + (o + 1) * 32, :] = one_hot(col & 511, pos)

    loop(16, 1, build_send)

    loads[0].wait()
    for l in range(layers):
        down = jnp.transpose(down_ref[l].astype(f32)).astype(bf16)
        for g in range(4):
            down_wide[l, :, g * 64 : (g + 1) * 64] = down

    def pre(l, g, v):
        inner_g = residual(v, pre_in_ref[l], pre_out_ref[l])
        inner[pl.ds(g * 512, 512), :] = inner_g
        proj = silu(dot(inner_g, down_wide[l])).astype(bf16)
        table[...] = jnp.where(group_id == g, proj, table[...])

    def first(g):
        pre(0, g, inner[pl.ds(g * 512, 512), :])

    table[...] = jnp.zeros_like(table)
    for copy in loads[1:4]:
        copy.wait()
    loop(4, 1, first)

    pl.semaphore_wait(barrier, peers - 1)

    def send_block(src, dst, peer, sem_index, recv):
        @pl.when(peer != me)
        def _():
            pltpu.make_async_remote_copy(
                src_ref=src,
                dst_ref=dst,
                send_sem=send_sem.at[sem_index],
                recv_sem=recv,
                device_id=(peer // atoms, lax.rem(peer, atoms)),
                device_id_type=MESH,
            ).start()

        @pl.when(peer == me)
        def _():
            pltpu.make_async_copy(src, dst, recv).start()

    def provide(l):
        def send_chunk(c):
            def one(o, carry):
                peer = c * 8 + o
                send_block(
                    payload.at[peer],
                    arrived.at[l, me // 2, lax.rem(me, 2)],
                    peer,
                    l * 2,
                    recv_sem.at[l * 8 + me // 32],
                )
                return carry

            lax.fori_loop(0, 8, one, 0)

        def compute(c):
            values = dot(pick_send[c], table[...])
            cols = col_send[c]
            for o in range(8):
                half = []
                for h in range(2):
                    low = cols[h * 32 : (h + 1) * 32, o : o + 1] >> 9
                    e = values[h * 256 + o * 32 : h * 256 + (o + 1) * 32]
                    v = jnp.where(low >= 2, e[:, 128:], e[:, :128])
                    half.append((v, pltpu.roll(v, 64, 1), (low & 1) == 1))
                (v0, w0, odd0), (v1, w1, odd1) = half
                picked = jnp.where(low_half, jnp.where(odd0, w0, v0), jnp.where(odd1, v1, w1))
                payload[c * 8 + o] = picked.astype(bf16)

        def chunk(step, carry):
            for u in range(2):
                compute(lax.rem(me // 8 + step * 2 + u, 16))

            @pl.when(step > 0)
            def _():
                for u in range(2):
                    send_chunk(lax.rem(me // 8 + step * 2 + u + 14, 16))

            return carry

        lax.fori_loop(0, 8, chunk, 0)
        for u in range(2):
            send_chunk(lax.rem(me // 8 + 14 + u, 16))

    def prepare():
        source_t = jnp.transpose(source_ref[...])
        target_t = jnp.transpose(target_ref[...])
        rows = lax.broadcasted_iota(i32, (128, 1), 0) // 32
        for c in range(16):
            col_source[c] = source_t[:, c : c + 1]
            t = target_t[:, c : c + 1]
            low = ((t >> 5) & 1) * 2 + ((t >> 4) & 1)
            col_target[c] = jnp.where(rows + c * 4 < count_ref[0], low, -1)

        def build_source(c):
            s = col_source[c]
            key = (s >> 7) * 32 + (s & 31)
            for k in range(4):
                pick_source[k, pl.ds(c * 128, 128), :] = one_hot(key, lanes((128, 512)) + k * 512)

        loop(16, 1, build_source)

        t = target_row_ref[...]
        target_key = (t >> 6) * 16 + (t & 15)

        def build_target(c):
            pos = lax.broadcasted_iota(i32, (64, 2048), 0) + c * 64
            pick_target[pl.ds(c * 64, 64), :] = one_hot(target_key, pos)

        loop(16, 1, build_target)

        loads[4].wait()

        def turn(g):
            block = basis_ref[pl.ds(g * 4, 4)].reshape(128, 512).astype(f32)
            turned[...] = jnp.transpose(block)
            for k in range(16):
                basis_t[g, k * 32 : (k + 1) * 32, :] = turned[pl.ds(k, 32, stride=16), :].astype(bf16)

        loop(16, 1, turn)

        loads[5].wait()
        bil_wide[...] = jnp.zeros_like(bil_wide)
        for l in range(layers):
            for k in range(16):
                if k % 2 == 0:
                    pair = jnp.transpose(bil_ref[l, :, k * 64 : k * 64 + 128].astype(f32)).astype(bf16)
                w = pair[k % 2 * 64 : k % 2 * 64 + 64]
                for b in range(4):
                    start = k * 256 + b * 64
                    bil_wide[l, start : start + 64, b * 64 : (b + 1) * 64] = w

    def prepare_return():
        return_t = jnp.transpose(return_ref[...])
        for c in range(32):
            col_return[c] = return_t[:, c : c + 1] >> 9
        return_key = return_row_ref[...] & 511

        def build_return(c):
            pos = lax.broadcasted_iota(i32, (64, 1024), 0) + c * 64
            for k in range(4):
                key = return_key[:, k * 1024 : (k + 1) * 1024]
                pick_return[k, pl.ds(c * 64, 64), :] = one_hot(key, pos)

        loop(8, 1, build_return)
        for copy in loads[6:]:
            copy.wait()
        for g in range(4):
            up_tall[g * 64 : (g + 1) * 64, :] = up_ref[0]

    def triplet(l):
        for n in range(4):
            k = lax.rem(me // 32 + 4 - n, 4)
            pltpu.make_async_copy(
                arrived.at[l, pl.ds(0, 16)], arrived.at[l, pl.ds(0, 16)], recv_sem.at[l * 8 + k]
            ).wait()
            block = jnp.concatenate(
                [
                    arrived[l, pl.ds(k * 16, 16), 0].reshape(512, 128),
                    arrived[l, pl.ds(k * 16, 16), 1].reshape(512, 128),
                ],
                axis=1,
            )

            def gather(m):
                part = dot(pick_source[k, pl.ds(m * 1024, 1024), :], block)
                if n > 0:
                    part = part + gathered[pl.ds(m * 1024, 1024), :]
                gathered[pl.ds(m * 1024, 1024), :] = part

            loop(2, 1, gather)

        row_block = lax.broadcasted_iota(i32, (128, 1), 0) // 32

        def contract(g):
            s = col_source[g]
            a = gathered[pl.ds(g * 128, 128), :]
            v = jnp.where(((s >> 6) & 1) == 1, a[:, 128:], a[:, :128])
            w = pltpu.roll(v, 64, 1)
            both = jnp.where(((s >> 5) & 1) != half_id, w, v)
            right = jnp.concatenate(
                [
                    jnp.where(row_block == half_id, both, 0.0),
                    jnp.where(row_block == half_id + 2, both, 0.0),
                ],
                axis=1,
            ).astype(bf16)
            c = dot(basis_t[g], right).astype(bf16)
            for k in range(16):
                mixed[pl.ds(g * 32, 32), k * 256 : (k + 1) * 256] = c[k * 32 : (k + 1) * 32]

        loop(16, 4, contract)

        partial[...] = dot(mixed[...], bil_wide[l])

        def scatter(g):
            p = partial[pl.ds(g * 32, 32), :]
            for half in range(2):
                v = p[:, half * 128 : (half + 1) * 128]
                w = pltpu.roll(v, 64, 1)
                for b in range(2):
                    both = jnp.where(low_half, v, w) if b == 0 else jnp.where(low_half, w, v)
                    b4 = half * 2 + b
                    low = col_target[g, b4 * 32 : (b4 + 1) * 32, :]
                    rows = pl.ds(g * 128 + b4 * 32, 32)
                    spread[rows, 0:128] = jnp.where(low == half_id, both, 0.0).astype(bf16)
                    spread[rows, 128:256] = jnp.where(low == half_id + 2, both, 0.0).astype(bf16)

        loop(16, 4, scatter)

    def give_back(l):
        def send_chunk(c):
            def one(i, carry):
                peer = c * 32 + i
                send_block(
                    outgoing.at[peer // 2, lax.rem(peer, 2)],
                    incoming.at[l, me],
                    peer,
                    l * 2 + 1,
                    recv_sem.at[l * 8 + 4 + me // 32],
                )
                return carry

            lax.fori_loop(0, 32, one, 0)

        def chunk(n, carry):
            c = lax.rem(me // 32 + n, 4)
            sums = dot(pick_target[pl.ds(c * 256, 256), :], spread[...]).astype(bf16)
            outgoing[pl.ds(c * 16, 16), 0] = sums[:, :128].reshape(16, 16, 128)
            outgoing[pl.ds(c * 16, 16), 1] = sums[:, 128:].reshape(16, 16, 128)

            @pl.when(n > 0)
            def _():
                send_chunk(lax.rem(me // 32 + n + 3, 4))

            return carry

        lax.fori_loop(0, 4, chunk, 0)
        send_chunk(lax.rem(me // 32 + 3, 4))

    def receive(l):
        for n in range(4):
            c = lax.rem(me // 32 + 4 - n, 4)
            pltpu.make_async_copy(
                incoming.at[l, pl.ds(0, 32)], incoming.at[l, pl.ds(0, 32)], recv_sem.at[l * 8 + 4 + c]
            ).wait()

            def place(q):
                for o in range(4):
                    v = incoming[l, c * 32 + q * 4 + o].astype(f32)
                    w = pltpu.roll(v, 64, 1)
                    for h in range(2):
                        both = jnp.where(low_half, v, w) if h == 0 else jnp.where(low_half, w, v)
                        low = col_return[c * 8 + q, o * 32 + h * 16 : o * 32 + (h + 1) * 16, :]
                        rows = pl.ds(q * 128 + o * 32 + h * 16, 16)
                        spread_in[rows, 0:128] = jnp.where(low == half_id, both, 0.0).astype(bf16)
                        spread_in[rows, 128:256] = jnp.where(low == half_id + 2, both, 0.0).astype(bf16)

            loop(8, 4, place)
            part = dot(pick_return[c], spread_in[...])
            if n > 0:
                part = part + message[...]
            message[...] = part

    def sent(rows, index):
        pltpu.make_async_copy(rows, rows, send_sem.at[index]).wait()

    for l in range(layers):
        provide(l)
        if l == 0:
            prepare()
        triplet(l)
        sent(payload.at[pl.ds(0, peers - 1)], l * 2)
        give_back(l)
        if l == 0:
            prepare_return()
        receive(l)
        sent(incoming.at[l, pl.ds(0, peers - 1)], l * 2 + 1)
        if l < layers - 1:
            message_ref[...] = message[...].astype(bf16)

            def middle(g):
                joined = join(g, inner[pl.ds(g * 512, 512), :], message_ref[...], up_tall[...])
                pre(l + 1, g, residual(joined, post_in_ref[...], post_out_ref[...]))

            loop(4, 1, middle)
            store.start()
        else:
            message_ref[...] = message[...].astype(bf16)
    store.wait()


def on_device(
    bond_states,
    block_counts,
    send_rows,
    source_slots,
    target_slots,
    return_rows,
    angular_basis,
    pre_inner,
    pre_outer,
    down_proj,
    bilinear,
    up_proj,
    post_inner,
    post_outer,
):
    vmem = pl.BlockSpec(memory_space=pltpu.VMEM)
    hbm = pl.BlockSpec(memory_space=pl.ANY)
    inner, message = pl.pallas_call(
        kernel,
        name="triplet",
        out_shape=(
            jax.ShapeDtypeStruct((2048, 512), bf16),
            jax.ShapeDtypeStruct((512, 256), bf16),
        ),
        in_specs=[pl.BlockSpec(memory_space=pltpu.SMEM)] + [vmem] * 6 + [hbm] * 9,
        out_specs=(hbm, vmem),
        scratch_shapes=[
            pltpu.VMEM((64, 32, 512), bf16),
            pltpu.VMEM((2, 512, 512), bf16),
            pltpu.VMEM((2, 512, 512), bf16),
            pltpu.VMEM((2, 64, 512), bf16),
            pltpu.VMEM((2, 64, 1024), bf16),
            pltpu.VMEM((2, 64, 512), bf16),
            pltpu.VMEM((512, 512), bf16),
            pltpu.VMEM((512, 512), bf16),
            pltpu.VMEM((2048, 512), bf16),
            pltpu.VMEM((2, 512, 256), bf16),
            pltpu.VMEM((256, 512), bf16),
            pltpu.VMEM((512, 256), bf16),
            pltpu.VMEM((16, 512, 512), bf16),
            pltpu.VMEM((16, 64, 8), i32),
            pltpu.VMEM((4, 2048, 512), bf16),
            pltpu.VMEM((16, 128, 1), i32),
            pltpu.VMEM((1024, 2048), bf16),
            pltpu.VMEM((16, 128, 1), i32),
            pltpu.VMEM((4, 512, 1024), bf16),
            pltpu.VMEM((32, 128, 1), i32),
            pltpu.VMEM((16, 512, 128), bf16),
            pltpu.VMEM((512, 128), f32),
            pltpu.VMEM((2, 4096, 256), bf16),
            pltpu.VMEM((128, 32, 128), bf16),
            pltpu.VMEM((2, 64, 2, 32, 128), bf16),
            pltpu.VMEM((2048, 256), f32),
            pltpu.VMEM((512, 4096), bf16),
            pltpu.VMEM((512, 256), f32),
            pltpu.VMEM((2048, 256), bf16),
            pltpu.VMEM((64, 2, 16, 128), bf16),
            pltpu.VMEM((2, 128, 16, 128), bf16),
            pltpu.VMEM((1024, 256), bf16),
            pltpu.VMEM((512, 256), f32),
            pltpu.SemaphoreType.DMA((4,)),
            pltpu.SemaphoreType.DMA((16,)),
            pltpu.SemaphoreType.DMA((10,)),
        ],
        compiler_params=pltpu.CompilerParams(
            collective_id=0, has_side_effects=True, vmem_limit_bytes=67043328
        ),
    )(
        block_counts,
        jnp.transpose(send_rows[0]),
        source_slots.reshape(16, 128),
        target_slots.reshape(16, 128),
        target_slots,
        return_rows.reshape(32, 128),
        return_rows,
        bond_states,
        angular_basis,
        pre_inner,
        pre_outer,
        jnp.swapaxes(down_proj, 1, 2),
        jnp.swapaxes(bilinear, 1, 2),
        up_proj,
        post_inner,
        post_outer,
    )
    last = pl.BlockSpec((1, 512, 512), lambda g: (1, 0, 0))
    return pl.pallas_call(
        final,
        name="final",
        grid=(4,),
        out_shape=jax.ShapeDtypeStruct((2048, 512), bf16),
        in_specs=[
            pl.BlockSpec((512, 512), lambda g: (g, 0)),
            pl.BlockSpec((512, 256), lambda g: (0, 0)),
            pl.BlockSpec((1, 64, 512), lambda g: (1, 0, 0)),
            last,
            last,
        ],
        out_specs=pl.BlockSpec((512, 512), lambda g: (g, 0)),
    )(inner, message, up_proj, post_inner, post_outer)


def solution(mesh):
    split = ("bond", "atom")
    in_specs = (
        P(split, None),
        P(split),
        P(split, None, None),
        P(split, None),
        P(split, None),
        P(split, None),
        P(split, None, None),
    ) + (P(),) * 7
    return jax.shard_map(
        on_device, mesh=mesh, in_specs=in_specs, out_specs=P(split, None), check_vma=False
    )
```

```python
import functools

import jax
import jax.numpy as jnp
from jax import lax
from jax.experimental import pallas as pl
from jax.experimental.pallas import tpu as pltpu
from jax.sharding import PartitionSpec as P

MESH = pl.DeviceIdType.MESH
root_half = 0.7071067811865476
bf16 = jnp.bfloat16
f32 = jnp.float32
i32 = jnp.int32


def dot(a, b):
    return jnp.dot(a, b, preferred_element_type=f32)


def silu(v):
    half = 0.5 * v
    return half * jnp.tanh(half) + half


def lanes(shape):
    return lax.broadcasted_iota(i32, shape, 1)


def one_hot(index, positions):
    return jnp.where(index == positions, 1.0, 0.0).astype(bf16)


def loop(count, unroll, body):
    def some(step, carry):
        for u in range(unroll):
            body(step * unroll + u)
        return carry

    if count == unroll:
        some(0, 0)
    else:
        lax.fori_loop(0, count // unroll, some, 0)


def residual(v, w_in, w_out):
    hidden = silu(dot(v, w_in)).astype(bf16)
    return ((v.astype(f32) + silu(dot(hidden, w_out))) * root_half).astype(bf16)


def join(g, inner_g, message, up_tall):
    group_id = lanes((1, 256)) // 64
    picked = jnp.where(group_id == g, message, jnp.zeros_like(message))
    added = silu(dot(picked, up_tall))
    return ((inner_g.astype(f32) + added) * root_half).astype(bf16)


def final(inner_ref, message_ref, up_ref, w_in_ref, w_out_ref, out_ref):
    up_tall = jnp.concatenate([up_ref[0]] * 4, axis=0)
    joined = join(pl.program_id(0), inner_ref[...], message_ref[...], up_tall)
    out_ref[...] = residual(joined, w_in_ref[0], w_out_ref[0])


def kernel(
    count_ref,
    send_ref,
    source_ref,
    target_ref,
    target_row_ref,
    return_ref,
    return_row_ref,
    x_hbm,
    basis_hbm,
    pre_in_hbm,
    pre_out_hbm,
    down_hbm,
    bil_hbm,
    up_hbm,
    post_in_hbm,
    post_out_hbm,
    inner_hbm,
    message_ref,
    basis_ref,
    pre_in_ref,
    pre_out_ref,
    down_ref,
    bil_ref,
    up_ref,
    post_in_ref,
    post_out_ref,
    inner,
    down_wide,
    up_tall,
    table,
    pick_send,
    col_send,
    pick_source,
    col_source,
    pick_target,
    col_target,
    pick_return,
    col_return,
    basis_t,
    turned,
    bil_wide,
    payload,
    arrived,
    gathered,
    mixed,
    partial,
    spread,
    outgoing,
    incoming,
    spread_in,
    message,
    send_sem,
    recv_sem,
    load_sem,
):
    me_bond = lax.axis_index("bond")
    me_atom = lax.axis_index("atom")
    atoms = 16
    peers = 128
    me = me_bond * atoms + me_atom
    layers = 2

    barrier = pltpu.get_barrier_semaphore()

    def greet(step, carry):
        peer = lax.rem(me + step, peers)
        pl.semaphore_signal(
            barrier, inc=1, device_id=(peer // atoms, lax.rem(peer, atoms)), device_id_type=MESH
        )
        return carry

    lax.fori_loop(1, peers, greet, 0)

    loads = [
        pltpu.make_async_copy(src, dst, load_sem.at[n])
        for n, (src, dst) in enumerate(
            (
                (down_hbm, down_ref),
                (pre_in_hbm, pre_in_ref),
                (pre_out_hbm, pre_out_ref),
                (x_hbm, inner),
                (basis_hbm, basis_ref),
                (bil_hbm, bil_ref),
                (up_hbm, up_ref),
                (post_in_hbm.at[0], post_in_ref),
                (post_out_hbm.at[0], post_out_ref),
            )
        )
    ]
    for copy in loads:
        copy.start()
    store = pltpu.make_async_copy(inner, inner_hbm, load_sem.at[len(loads)])

    lane128 = lanes((1, 128))
    low_half = lane128 < 64
    half_id = lane128 // 64
    lane256 = lanes((1, 256))
    group_id = lane256 // 64

    for c in range(16):
        col_send[c] = send_ref[:, c * 8 : (c + 1) * 8]

    def build_send(c):
        cols = col_send[c]
        pos = lanes((32, 512))
        for h in range(2):
            for o in range(8):
                col = cols[h * 32 : (h + 1) * 32, o : o + 1]
                pick_send[c, h * 256 + o * 32 : h * 256 + (o + 1) * 32, :] = one_hot(col & 511, pos)

    loop(16, 1, build_send)

    loads[0].wait()
    for l in range(layers):
        down = jnp.transpose(down_ref[l].astype(f32)).astype(bf16)
        for g in range(4):
            down_wide[l, :, g * 64 : (g + 1) * 64] = down

    def pre(l, g, v):
        inner_g = residual(v, pre_in_ref[l], pre_out_ref[l])
        inner[pl.ds(g * 512, 512), :] = inner_g
        proj = silu(dot(inner_g, down_wide[l])).astype(bf16)
        table[...] = jnp.where(group_id == g, proj, table[...])

    def first(g):
        pre(0, g, inner[pl.ds(g * 512, 512), :])

    table[...] = jnp.zeros_like(table)
    for copy in loads[1:4]:
        copy.wait()
    loop(4, 1, first)

    pl.semaphore_wait(barrier, peers - 1)

    def send_block(src, dst, peer, sem_index, recv):
        @pl.when(peer != me)
        def _():
            pltpu.make_async_remote_copy(
                src_ref=src,
                dst_ref=dst,
                send_sem=send_sem.at[sem_index],
                recv_sem=recv,
                device_id=(peer // atoms, lax.rem(peer, atoms)),
                device_id_type=MESH,
            ).start()

        @pl.when(peer == me)
        def _():
            pltpu.make_async_copy(src, dst, recv).start()

    def provide(l):
        def send_chunk(c):
            def one(o, carry):
                peer = c * 8 + lax.rem(me + o, 8)
                send_block(
                    payload.at[peer],
                    arrived.at[l, me // 2, lax.rem(me, 2)],
                    peer,
                    l * 2,
                    recv_sem.at[l * 8 + me // 32],
                )
                return carry

            lax.fori_loop(0, 8, one, 0)

        def compute(c):
            values = dot(pick_send[c], table[...])
            cols = col_send[c]
            for o in range(8):
                half = []
                for h in range(2):
                    low = cols[h * 32 : (h + 1) * 32, o : o + 1] >> 9
                    e = values[h * 256 + o * 32 : h * 256 + (o + 1) * 32]
                    v = jnp.where(low >= 2, e[:, 128:], e[:, :128])
                    half.append((v, pltpu.roll(v, 64, 1), (low & 1) == 1))
                (v0, w0, odd0), (v1, w1, odd1) = half
                picked = jnp.where(low_half, jnp.where(odd0, w0, v0), jnp.where(odd1, v1, w1))
                payload[c * 8 + o] = picked.astype(bf16)

        def chunk(step, carry):
            for u in range(2):
                compute(lax.rem(me // 8 + step * 2 + u, 16))

            @pl.when(step > 0)
            def _():
                for u in range(2):
                    send_chunk(lax.rem(me // 8 + step * 2 + u + 14, 16))

            return carry

        lax.fori_loop(0, 8, chunk, 0)
        for u in range(2):
            send_chunk(lax.rem(me // 8 + 14 + u, 16))

    def prepare():
        source_t = jnp.transpose(source_ref[...])
        target_t = jnp.transpose(target_ref[...])
        rows = lax.broadcasted_iota(i32, (128, 1), 0) // 32
        for c in range(16):
            col_source[c] = source_t[:, c : c + 1]
            t = target_t[:, c : c + 1]
            low = ((t >> 5) & 1) * 2 + ((t >> 4) & 1)
            col_target[c] = jnp.where(rows + c * 4 < count_ref[0], low, -1)

        def build_source(c):
            s = col_source[c]
            key = (s >> 7) * 32 + (s & 31)
            for k in range(4):
                pick_source[k, pl.ds(c * 128, 128), :] = one_hot(key, lanes((128, 512)) + k * 512)

        loop(16, 1, build_source)

        t = target_row_ref[...]
        target_key = (t >> 6) * 16 + (t & 15)

        def build_target(c):
            pos = lax.broadcasted_iota(i32, (64, 2048), 0) + c * 64
            pick_target[pl.ds(c * 64, 64), :] = one_hot(target_key, pos)

        loop(16, 1, build_target)

        loads[4].wait()

        def turn(g):
            block = basis_ref[pl.ds(g * 4, 4)].reshape(128, 512).astype(f32)
            turned[...] = jnp.transpose(block)
            for k in range(16):
                basis_t[g, k * 32 : (k + 1) * 32, :] = turned[pl.ds(k, 32, stride=16), :].astype(bf16)

        loop(16, 1, turn)

        loads[5].wait()
        bil_wide[...] = jnp.zeros_like(bil_wide)
        for l in range(layers):
            for k in range(16):
                if k % 2 == 0:
                    pair = jnp.transpose(bil_ref[l, :, k * 64 : k * 64 + 128].astype(f32)).astype(bf16)
                w = pair[k % 2 * 64 : k % 2 * 64 + 64]
                for b in range(4):
                    start = k * 256 + b * 64
                    bil_wide[l, start : start + 64, b * 64 : (b + 1) * 64] = w

    def prepare_return():
        return_t = jnp.transpose(return_ref[...])
        for c in range(32):
            col_return[c] = return_t[:, c : c + 1] >> 9
        return_key = return_row_ref[...] & 511

        def build_return(c):
            pos = lax.broadcasted_iota(i32, (64, 1024), 0) + c * 64
            for k in range(4):
                key = return_key[:, k * 1024 : (k + 1) * 1024]
                pick_return[k, pl.ds(c * 64, 64), :] = one_hot(key, pos)

        loop(8, 1, build_return)
        for copy in loads[6:]:
            copy.wait()
        for g in range(4):
            up_tall[g * 64 : (g + 1) * 64, :] = up_ref[0]

    def triplet(l):
        for n in range(4):
            k = lax.rem(me // 32 + 4 - n, 4)
            pltpu.make_async_copy(
                arrived.at[l, pl.ds(0, 16)], arrived.at[l, pl.ds(0, 16)], recv_sem.at[l * 8 + k]
            ).wait()
            block = jnp.concatenate(
                [
                    arrived[l, pl.ds(k * 16, 16), 0].reshape(512, 128),
                    arrived[l, pl.ds(k * 16, 16), 1].reshape(512, 128),
                ],
                axis=1,
            )

            def gather(m):
                part = dot(pick_source[k, pl.ds(m * 1024, 1024), :], block)
                if n > 0:
                    part = part + gathered[pl.ds(m * 1024, 1024), :]
                gathered[pl.ds(m * 1024, 1024), :] = part

            loop(2, 1, gather)

        row_block = lax.broadcasted_iota(i32, (128, 1), 0) // 32

        def contract(g):
            s = col_source[g]
            a = gathered[pl.ds(g * 128, 128), :]
            v = jnp.where(((s >> 6) & 1) == 1, a[:, 128:], a[:, :128])
            w = pltpu.roll(v, 64, 1)
            both = jnp.where(((s >> 5) & 1) != half_id, w, v)
            right = jnp.concatenate(
                [
                    jnp.where(row_block == half_id, both, 0.0),
                    jnp.where(row_block == half_id + 2, both, 0.0),
                ],
                axis=1,
            ).astype(bf16)
            c = dot(basis_t[g], right).astype(bf16)
            for k in range(16):
                mixed[pl.ds(g * 32, 32), k * 256 : (k + 1) * 256] = c[k * 32 : (k + 1) * 32]

        loop(16, 8, contract)

        partial[...] = dot(mixed[...], bil_wide[l])

        def scatter(g):
            p = partial[pl.ds(g * 32, 32), :]
            for half in range(2):
                v = p[:, half * 128 : (half + 1) * 128]
                w = pltpu.roll(v, 64, 1)
                for b in range(2):
                    both = jnp.where(low_half, v, w) if b == 0 else jnp.where(low_half, w, v)
                    b4 = half * 2 + b
                    low = col_target[g, b4 * 32 : (b4 + 1) * 32, :]
                    rows = pl.ds(g * 128 + b4 * 32, 32)
                    spread[rows, 0:128] = jnp.where(low == half_id, both, 0.0).astype(bf16)
                    spread[rows, 128:256] = jnp.where(low == half_id + 2, both, 0.0).astype(bf16)

        loop(16, 4, scatter)

    def give_back(l):
        def send_chunk(c):
            def one(i, carry):
                peer = c * 32 + lax.rem(me + i, 32)
                send_block(
                    outgoing.at[peer // 2, lax.rem(peer, 2)],
                    incoming.at[l, me],
                    peer,
                    l * 2 + 1,
                    recv_sem.at[l * 8 + 4 + me // 32],
                )
                return carry

            lax.fori_loop(0, 32, one, 0)

        def chunk(n, carry):
            c = lax.rem(me // 32 + n, 4)
            sums = dot(pick_target[pl.ds(c * 256, 256), :], spread[...]).astype(bf16)
            outgoing[pl.ds(c * 16, 16), 0] = sums[:, :128].reshape(16, 16, 128)
            outgoing[pl.ds(c * 16, 16), 1] = sums[:, 128:].reshape(16, 16, 128)

            @pl.when(n > 0)
            def _():
                send_chunk(lax.rem(me // 32 + n + 3, 4))

            return carry

        lax.fori_loop(0, 4, chunk, 0)
        send_chunk(lax.rem(me // 32 + 3, 4))

    def receive(l):
        for n in range(4):
            c = lax.rem(me // 32 + 4 - n, 4)
            pltpu.make_async_copy(
                incoming.at[l, pl.ds(0, 32)], incoming.at[l, pl.ds(0, 32)], recv_sem.at[l * 8 + 4 + c]
            ).wait()

            def place(q):
                for o in range(4):
                    v = incoming[l, c * 32 + q * 4 + o].astype(f32)
                    w = pltpu.roll(v, 64, 1)
                    for h in range(2):
                        both = jnp.where(low_half, v, w) if h == 0 else jnp.where(low_half, w, v)
                        low = col_return[c * 8 + q, o * 32 + h * 16 : o * 32 + (h + 1) * 16, :]
                        rows = pl.ds(q * 128 + o * 32 + h * 16, 16)
                        spread_in[rows, 0:128] = jnp.where(low == half_id, both, 0.0).astype(bf16)
                        spread_in[rows, 128:256] = jnp.where(low == half_id + 2, both, 0.0).astype(bf16)

            loop(8, 4, place)
            part = dot(pick_return[c], spread_in[...])
            if n > 0:
                part = part + message[...]
            message[...] = part

    def sent(rows, index):
        pltpu.make_async_copy(rows, rows, send_sem.at[index]).wait()

    for l in range(layers):
        provide(l)
        if l == 0:
            prepare()
        triplet(l)
        sent(payload.at[pl.ds(0, peers - 1)], l * 2)
        give_back(l)
        if l == 0:
            prepare_return()
        receive(l)
        sent(incoming.at[l, pl.ds(0, peers - 1)], l * 2 + 1)
        if l < layers - 1:
            message_ref[...] = message[...].astype(bf16)

            def middle(g):
                joined = join(g, inner[pl.ds(g * 512, 512), :], message_ref[...], up_tall[...])
                pre(l + 1, g, residual(joined, post_in_ref[...], post_out_ref[...]))

            loop(4, 1, middle)
            store.start()
        else:
            message_ref[...] = message[...].astype(bf16)
    store.wait()


def on_device(
    bond_states,
    block_counts,
    send_rows,
    source_slots,
    target_slots,
    return_rows,
    angular_basis,
    pre_inner,
    pre_outer,
    down_proj,
    bilinear,
    up_proj,
    post_inner,
    post_outer,
):
    vmem = pl.BlockSpec(memory_space=pltpu.VMEM)
    hbm = pl.BlockSpec(memory_space=pl.ANY)
    inner, message = pl.pallas_call(
        kernel,
        name="triplet",
        out_shape=(
            jax.ShapeDtypeStruct((2048, 512), bf16),
            jax.ShapeDtypeStruct((512, 256), bf16),
        ),
        in_specs=[pl.BlockSpec(memory_space=pltpu.SMEM)] + [vmem] * 6 + [hbm] * 9,
        out_specs=(hbm, vmem),
        scratch_shapes=[
            pltpu.VMEM((64, 32, 512), bf16),
            pltpu.VMEM((2, 512, 512), bf16),
            pltpu.VMEM((2, 512, 512), bf16),
            pltpu.VMEM((2, 64, 512), bf16),
            pltpu.VMEM((2, 64, 1024), bf16),
            pltpu.VMEM((2, 64, 512), bf16),
            pltpu.VMEM((512, 512), bf16),
            pltpu.VMEM((512, 512), bf16),
            pltpu.VMEM((2048, 512), bf16),
            pltpu.VMEM((2, 512, 256), bf16),
            pltpu.VMEM((256, 512), bf16),
            pltpu.VMEM((512, 256), bf16),
            pltpu.VMEM((16, 512, 512), bf16),
            pltpu.VMEM((16, 64, 8), i32),
            pltpu.VMEM((4, 2048, 512), bf16),
            pltpu.VMEM((16, 128, 1), i32),
            pltpu.VMEM((1024, 2048), bf16),
            pltpu.VMEM((16, 128, 1), i32),
            pltpu.VMEM((4, 512, 1024), bf16),
            pltpu.VMEM((32, 128, 1), i32),
            pltpu.VMEM((16, 512, 128), bf16),
            pltpu.VMEM((512, 128), f32),
            pltpu.VMEM((2, 4096, 256), bf16),
            pltpu.VMEM((128, 32, 128), bf16),
            pltpu.VMEM((2, 64, 2, 32, 128), bf16),
            pltpu.VMEM((2048, 256), f32),
            pltpu.VMEM((512, 4096), bf16),
            pltpu.VMEM((512, 256), f32),
            pltpu.VMEM((2048, 256), bf16),
            pltpu.VMEM((64, 2, 16, 128), bf16),
            pltpu.VMEM((2, 128, 16, 128), bf16),
            pltpu.VMEM((1024, 256), bf16),
            pltpu.VMEM((512, 256), f32),
            pltpu.SemaphoreType.DMA((4,)),
            pltpu.SemaphoreType.DMA((16,)),
            pltpu.SemaphoreType.DMA((10,)),
        ],
        compiler_params=pltpu.CompilerParams(
            collective_id=0, has_side_effects=True, vmem_limit_bytes=67043328
        ),
    )(
        block_counts,
        jnp.transpose(send_rows[0]),
        source_slots.reshape(16, 128),
        target_slots.reshape(16, 128),
        target_slots,
        return_rows.reshape(32, 128),
        return_rows,
        bond_states,
        angular_basis,
        pre_inner,
        pre_outer,
        jnp.swapaxes(down_proj, 1, 2),
        jnp.swapaxes(bilinear, 1, 2),
        up_proj,
        post_inner,
        post_outer,
    )
    last = pl.BlockSpec((1, 512, 512), lambda g: (1, 0, 0))
    return pl.pallas_call(
        final,
        name="final",
        grid=(4,),
        out_shape=jax.ShapeDtypeStruct((2048, 512), bf16),
        in_specs=[
            pl.BlockSpec((512, 512), lambda g: (g, 0)),
            pl.BlockSpec((512, 256), lambda g: (0, 0)),
            pl.BlockSpec((1, 64, 512), lambda g: (1, 0, 0)),
            last,
            last,
        ],
        out_specs=pl.BlockSpec((512, 512), lambda g: (g, 0)),
    )(inner, message, up_proj, post_inner, post_outer)


def solution(mesh):
    split = ("bond", "atom")
    in_specs = (
        P(split, None),
        P(split),
        P(split, None, None),
        P(split, None),
        P(split, None),
        P(split, None),
        P(split, None, None),
    ) + (P(),) * 7
    return jax.shard_map(
        on_device, mesh=mesh, in_specs=in_specs, out_specs=P(split, None), check_vma=False
    )
```

```python
import functools

import jax
import jax.numpy as jnp
from jax import lax
from jax.experimental import pallas as pl
from jax.experimental.pallas import tpu as pltpu
from jax.sharding import PartitionSpec as P

MESH = pl.DeviceIdType.MESH
root_half = 0.7071067811865476
bf16 = jnp.bfloat16
f32 = jnp.float32
i32 = jnp.int32


def dot(a, b):
    return jnp.dot(a, b, preferred_element_type=f32)


def silu(v):
    half = 0.5 * v
    return half * jnp.tanh(half) + half


def lanes(shape):
    return lax.broadcasted_iota(i32, shape, 1)


def one_hot(index, positions):
    return jnp.where(index == positions, 1.0, 0.0).astype(bf16)


def loop(count, unroll, body):
    def some(step, carry):
        for u in range(unroll):
            body(step * unroll + u)
        return carry

    if count == unroll:
        some(0, 0)
    else:
        lax.fori_loop(0, count // unroll, some, 0)


def residual(v, w_in, w_out):
    hidden = silu(dot(v, w_in)).astype(bf16)
    return ((v.astype(f32) + silu(dot(hidden, w_out))) * root_half).astype(bf16)


def join(g, inner_g, message, up_tall):
    group_id = lanes((1, 256)) // 64
    picked = jnp.where(group_id == g, message, jnp.zeros_like(message))
    added = silu(dot(picked, up_tall))
    return ((inner_g.astype(f32) + added) * root_half).astype(bf16)


def final(inner_ref, message_ref, up_ref, w_in_ref, w_out_ref, out_ref):
    up_tall = jnp.concatenate([up_ref[0]] * 4, axis=0)
    joined = join(pl.program_id(0), inner_ref[...], message_ref[...], up_tall)
    out_ref[...] = residual(joined, w_in_ref[0], w_out_ref[0])


def kernel(
    count_ref,
    send_ref,
    source_ref,
    target_ref,
    target_row_ref,
    return_ref,
    return_row_ref,
    x_hbm,
    basis_hbm,
    pre_in_hbm,
    pre_out_hbm,
    down_hbm,
    bil_hbm,
    up_hbm,
    post_in_hbm,
    post_out_hbm,
    inner_hbm,
    message_ref,
    basis_ref,
    pre_in_ref,
    pre_out_ref,
    down_ref,
    bil_ref,
    up_ref,
    post_in_ref,
    post_out_ref,
    inner,
    down_wide,
    up_tall,
    table,
    pick_send,
    col_send,
    pick_source,
    col_source,
    pick_target,
    col_target,
    pick_return,
    col_return,
    basis_t,
    turned,
    bil_wide,
    payload,
    arrived,
    gathered,
    mixed,
    partial,
    spread,
    outgoing,
    incoming,
    spread_in,
    message,
    send_sem,
    recv_sem,
    load_sem,
    meet_sem,
):
    me_bond = lax.axis_index("bond")
    me_atom = lax.axis_index("atom")
    atoms = 16
    peers = 128
    me = me_bond * atoms + me_atom
    layers = 2

    barrier = pltpu.get_barrier_semaphore()

    def greet(semaphore, bond, atom):
        pl.semaphore_signal(semaphore, inc=1, device_id=(bond, atom), device_id_type=MESH)

    bonds = peers // atoms
    for step in range(1, atoms):
        greet(barrier, me_bond, lax.rem(me_atom + step, atoms))
    for step in range(1, bonds):
        greet(barrier, lax.rem(me_bond + step, bonds), me_atom)

    loads = [
        pltpu.make_async_copy(src, dst, load_sem.at[n])
        for n, (src, dst) in enumerate(
            (
                (down_hbm, down_ref),
                (pre_in_hbm, pre_in_ref),
                (pre_out_hbm, pre_out_ref),
                (x_hbm, inner),
                (basis_hbm, basis_ref),
                (bil_hbm, bil_ref),
                (up_hbm, up_ref),
                (post_in_hbm.at[0], post_in_ref),
                (post_out_hbm.at[0], post_out_ref),
            )
        )
    ]
    for copy in loads:
        copy.start()
    store = pltpu.make_async_copy(inner, inner_hbm, load_sem.at[len(loads)])

    lane128 = lanes((1, 128))
    low_half = lane128 < 64
    half_id = lane128 // 64
    lane256 = lanes((1, 256))
    group_id = lane256 // 64

    for c in range(16):
        col_send[c] = send_ref[:, c * 8 : (c + 1) * 8]

    def build_send(c):
        cols = col_send[c]
        pos = lanes((32, 512))
        for h in range(2):
            for o in range(8):
                col = cols[h * 32 : (h + 1) * 32, o : o + 1]
                pick_send[c, h * 256 + o * 32 : h * 256 + (o + 1) * 32, :] = one_hot(col & 511, pos)

    loop(16, 1, build_send)
    pl.semaphore_wait(barrier, atoms + bonds - 2)
    for step in range(1, bonds):
        greet(meet_sem, lax.rem(me_bond + step, bonds), me_atom)


    loads[0].wait()
    for l in range(layers):
        down = jnp.transpose(down_ref[l].astype(f32)).astype(bf16)
        for g in range(4):
            down_wide[l, :, g * 64 : (g + 1) * 64] = down

    def pre(l, g, v):
        inner_g = residual(v, pre_in_ref[l], pre_out_ref[l])
        inner[pl.ds(g * 512, 512), :] = inner_g
        proj = silu(dot(inner_g, down_wide[l])).astype(bf16)
        table[...] = jnp.where(group_id == g, proj, table[...])

    def first(g):
        pre(0, g, inner[pl.ds(g * 512, 512), :])

    table[...] = jnp.zeros_like(table)
    for copy in loads[1:4]:
        copy.wait()
    loop(4, 1, first)

    pl.semaphore_wait(meet_sem, bonds - 1)

    def send_block(src, dst, peer, sem_index, recv):
        @pl.when(peer != me)
        def _():
            pltpu.make_async_remote_copy(
                src_ref=src,
                dst_ref=dst,
                send_sem=send_sem.at[sem_index],
                recv_sem=recv,
                device_id=(peer // atoms, lax.rem(peer, atoms)),
                device_id_type=MESH,
            ).start()

        @pl.when(peer == me)
        def _():
            pltpu.make_async_copy(src, dst, recv).start()

    def provide(l):
        def send_chunk(c):
            def one(o, carry):
                peer = c * 8 + lax.rem(me + o, 8)
                send_block(
                    payload.at[peer],
                    arrived.at[l, me // 2, lax.rem(me, 2)],
                    peer,
                    l * 2,
                    recv_sem.at[l * 8 + me // 32],
                )
                return carry

            lax.fori_loop(0, 8, one, 0)

        def compute(c):
            values = dot(pick_send[c], table[...])
            cols = col_send[c]
            for o in range(8):
                half = []
                for h in range(2):
                    low = cols[h * 32 : (h + 1) * 32, o : o + 1] >> 9
                    e = values[h * 256 + o * 32 : h * 256 + (o + 1) * 32]
                    v = jnp.where(low >= 2, e[:, 128:], e[:, :128])
                    half.append((v, pltpu.roll(v, 64, 1), (low & 1) == 1))
                (v0, w0, odd0), (v1, w1, odd1) = half
                picked = jnp.where(low_half, jnp.where(odd0, w0, v0), jnp.where(odd1, v1, w1))
                payload[c * 8 + o] = picked.astype(bf16)

        def chunk(step, carry):
            for u in range(2):
                compute(lax.rem(me // 8 + step * 2 + u, 16))

            @pl.when(step > 0)
            def _():
                for u in range(2):
                    send_chunk(lax.rem(me // 8 + step * 2 + u + 14, 16))

            return carry

        lax.fori_loop(0, 8, chunk, 0)
        for u in range(2):
            send_chunk(lax.rem(me // 8 + 14 + u, 16))

    def prepare():
        source_t = jnp.transpose(source_ref[...])
        target_t = jnp.transpose(target_ref[...])
        rows = lax.broadcasted_iota(i32, (128, 1), 0) // 32
        for c in range(16):
            col_source[c] = source_t[:, c : c + 1]
            t = target_t[:, c : c + 1]
            low = ((t >> 5) & 1) * 2 + ((t >> 4) & 1)
            col_target[c] = jnp.where(rows + c * 4 < count_ref[0], low, -1)

        def build_source(c):
            s = col_source[c]
            key = (s >> 7) * 32 + (s & 31)
            for k in range(4):
                pick_source[k, pl.ds(c * 128, 128), :] = one_hot(key, lanes((128, 512)) + k * 512)

        loop(16, 1, build_source)

        t = target_row_ref[...]
        target_key = (t >> 6) * 16 + (t & 15)

        def build_target(c):
            pos = lax.broadcasted_iota(i32, (64, 2048), 0) + c * 64
            pick_target[pl.ds(c * 64, 64), :] = one_hot(target_key, pos)

        loop(16, 1, build_target)

        loads[4].wait()

        def turn(g):
            block = basis_ref[pl.ds(g * 4, 4)].reshape(128, 512).astype(f32)
            turned[...] = jnp.transpose(block)
            for k in range(16):
                basis_t[g, k * 32 : (k + 1) * 32, :] = turned[pl.ds(k, 32, stride=16), :].astype(bf16)

        loop(16, 1, turn)

        loads[5].wait()
        bil_wide[...] = jnp.zeros_like(bil_wide)
        for l in range(layers):
            for k in range(16):
                if k % 2 == 0:
                    pair = jnp.transpose(bil_ref[l, :, k * 64 : k * 64 + 128].astype(f32)).astype(bf16)
                w = pair[k % 2 * 64 : k % 2 * 64 + 64]
                for b in range(4):
                    start = k * 256 + b * 64
                    bil_wide[l, start : start + 64, b * 64 : (b + 1) * 64] = w

    def prepare_return():
        return_t = jnp.transpose(return_ref[...])
        for c in range(32):
            col_return[c] = return_t[:, c : c + 1] >> 9
        return_key = return_row_ref[...] & 511

        def build_return(c):
            pos = lax.broadcasted_iota(i32, (64, 1024), 0) + c * 64
            for k in range(4):
                key = return_key[:, k * 1024 : (k + 1) * 1024]
                pick_return[k, pl.ds(c * 64, 64), :] = one_hot(key, pos)

        loop(8, 1, build_return)
        for copy in loads[6:]:
            copy.wait()
        for g in range(4):
            up_tall[g * 64 : (g + 1) * 64, :] = up_ref[0]

    def triplet(l):
        for n in range(4):
            k = lax.rem(me // 32 + 4 - n, 4)
            pltpu.make_async_copy(
                arrived.at[l, pl.ds(0, 16)], arrived.at[l, pl.ds(0, 16)], recv_sem.at[l * 8 + k]
            ).wait()
            block = jnp.concatenate(
                [
                    arrived[l, pl.ds(k * 16, 16), 0].reshape(512, 128),
                    arrived[l, pl.ds(k * 16, 16), 1].reshape(512, 128),
                ],
                axis=1,
            )

            def gather(m):
                part = dot(pick_source[k, pl.ds(m * 1024, 1024), :], block)
                if n > 0:
                    part = part + gathered[pl.ds(m * 1024, 1024), :]
                gathered[pl.ds(m * 1024, 1024), :] = part

            loop(2, 1, gather)

        row_block = lax.broadcasted_iota(i32, (128, 1), 0) // 32

        def contract(g):
            s = col_source[g]
            a = gathered[pl.ds(g * 128, 128), :]
            v = jnp.where(((s >> 6) & 1) == 1, a[:, 128:], a[:, :128])
            w = pltpu.roll(v, 64, 1)
            both = jnp.where(((s >> 5) & 1) != half_id, w, v)
            right = jnp.concatenate(
                [
                    jnp.where(row_block == half_id, both, 0.0),
                    jnp.where(row_block == half_id + 2, both, 0.0),
                ],
                axis=1,
            ).astype(bf16)
            c = dot(basis_t[g], right).astype(bf16)
            for k in range(16):
                mixed[pl.ds(g * 32, 32), k * 256 : (k + 1) * 256] = c[k * 32 : (k + 1) * 32]

        loop(16, 8, contract)

        partial[...] = dot(mixed[...], bil_wide[l])

        def scatter(g):
            p = partial[pl.ds(g * 32, 32), :]
            for half in range(2):
                v = p[:, half * 128 : (half + 1) * 128]
                w = pltpu.roll(v, 64, 1)
                for b in range(2):
                    both = jnp.where(low_half, v, w) if b == 0 else jnp.where(low_half, w, v)
                    b4 = half * 2 + b
                    low = col_target[g, b4 * 32 : (b4 + 1) * 32, :]
                    rows = pl.ds(g * 128 + b4 * 32, 32)
                    spread[rows, 0:128] = jnp.where(low == half_id, both, 0.0).astype(bf16)
                    spread[rows, 128:256] = jnp.where(low == half_id + 2, both, 0.0).astype(bf16)

        loop(16, 4, scatter)

    def give_back(l):
        def send_chunk(c):
            def one(i, carry):
                peer = c * 32 + lax.rem(me + i, 32)
                send_block(
                    outgoing.at[peer // 2, lax.rem(peer, 2)],
                    incoming.at[l, me],
                    peer,
                    l * 2 + 1,
                    recv_sem.at[l * 8 + 4 + me // 32],
                )
                return carry

            lax.fori_loop(0, 32, one, 0)

        def chunk(n, carry):
            c = lax.rem(me // 32 + n, 4)
            sums = dot(pick_target[pl.ds(c * 256, 256), :], spread[...]).astype(bf16)
            outgoing[pl.ds(c * 16, 16), 0] = sums[:, :128].reshape(16, 16, 128)
            outgoing[pl.ds(c * 16, 16), 1] = sums[:, 128:].reshape(16, 16, 128)

            @pl.when(n > 0)
            def _():
                send_chunk(lax.rem(me // 32 + n + 3, 4))

            return carry

        lax.fori_loop(0, 4, chunk, 0)
        send_chunk(lax.rem(me // 32 + 3, 4))

    def receive(l):
        for n in range(4):
            c = lax.rem(me // 32 + 4 - n, 4)
            pltpu.make_async_copy(
                incoming.at[l, pl.ds(0, 32)], incoming.at[l, pl.ds(0, 32)], recv_sem.at[l * 8 + 4 + c]
            ).wait()

            def place(q):
                for o in range(4):
                    v = incoming[l, c * 32 + q * 4 + o].astype(f32)
                    w = pltpu.roll(v, 64, 1)
                    for h in range(2):
                        both = jnp.where(low_half, v, w) if h == 0 else jnp.where(low_half, w, v)
                        low = col_return[c * 8 + q, o * 32 + h * 16 : o * 32 + (h + 1) * 16, :]
                        rows = pl.ds(q * 128 + o * 32 + h * 16, 16)
                        spread_in[rows, 0:128] = jnp.where(low == half_id, both, 0.0).astype(bf16)
                        spread_in[rows, 128:256] = jnp.where(low == half_id + 2, both, 0.0).astype(bf16)

            loop(8, 4, place)
            part = dot(pick_return[c], spread_in[...])
            if n > 0:
                part = part + message[...]
            message[...] = part

    def sent(rows, index):
        pltpu.make_async_copy(rows, rows, send_sem.at[index]).wait()

    for l in range(layers):
        provide(l)
        if l == 0:
            prepare()
        triplet(l)
        sent(payload.at[pl.ds(0, peers - 1)], l * 2)
        give_back(l)
        if l == 0:
            prepare_return()
        receive(l)
        sent(incoming.at[l, pl.ds(0, peers - 1)], l * 2 + 1)
        if l < layers - 1:
            message_ref[...] = message[...].astype(bf16)

            def middle(g):
                joined = join(g, inner[pl.ds(g * 512, 512), :], message_ref[...], up_tall[...])
                pre(l + 1, g, residual(joined, post_in_ref[...], post_out_ref[...]))

            loop(4, 1, middle)
            store.start()
        else:
            message_ref[...] = message[...].astype(bf16)
    store.wait()


def on_device(
    bond_states,
    block_counts,
    send_rows,
    source_slots,
    target_slots,
    return_rows,
    angular_basis,
    pre_inner,
    pre_outer,
    down_proj,
    bilinear,
    up_proj,
    post_inner,
    post_outer,
):
    vmem = pl.BlockSpec(memory_space=pltpu.VMEM)
    hbm = pl.BlockSpec(memory_space=pl.ANY)
    inner, message = pl.pallas_call(
        kernel,
        name="triplet",
        out_shape=(
            jax.ShapeDtypeStruct((2048, 512), bf16),
            jax.ShapeDtypeStruct((512, 256), bf16),
        ),
        in_specs=[pl.BlockSpec(memory_space=pltpu.SMEM)] + [vmem] * 6 + [hbm] * 9,
        out_specs=(hbm, vmem),
        scratch_shapes=[
            pltpu.VMEM((64, 32, 512), bf16),
            pltpu.VMEM((2, 512, 512), bf16),
            pltpu.VMEM((2, 512, 512), bf16),
            pltpu.VMEM((2, 64, 512), bf16),
            pltpu.VMEM((2, 64, 1024), bf16),
            pltpu.VMEM((2, 64, 512), bf16),
            pltpu.VMEM((512, 512), bf16),
            pltpu.VMEM((512, 512), bf16),
            pltpu.VMEM((2048, 512), bf16),
            pltpu.VMEM((2, 512, 256), bf16),
            pltpu.VMEM((256, 512), bf16),
            pltpu.VMEM((512, 256), bf16),
            pltpu.VMEM((16, 512, 512), bf16),
            pltpu.VMEM((16, 64, 8), i32),
            pltpu.VMEM((4, 2048, 512), bf16),
            pltpu.VMEM((16, 128, 1), i32),
            pltpu.VMEM((1024, 2048), bf16),
            pltpu.VMEM((16, 128, 1), i32),
            pltpu.VMEM((4, 512, 1024), bf16),
            pltpu.VMEM((32, 128, 1), i32),
            pltpu.VMEM((16, 512, 128), bf16),
            pltpu.VMEM((512, 128), f32),
            pltpu.VMEM((2, 4096, 256), bf16),
            pltpu.VMEM((128, 32, 128), bf16),
            pltpu.VMEM((2, 64, 2, 32, 128), bf16),
            pltpu.VMEM((2048, 256), f32),
            pltpu.VMEM((512, 4096), bf16),
            pltpu.VMEM((512, 256), f32),
            pltpu.VMEM((2048, 256), bf16),
            pltpu.VMEM((64, 2, 16, 128), bf16),
            pltpu.VMEM((2, 128, 16, 128), bf16),
            pltpu.VMEM((1024, 256), bf16),
            pltpu.VMEM((512, 256), f32),
            pltpu.SemaphoreType.DMA((4,)),
            pltpu.SemaphoreType.DMA((16,)),
            pltpu.SemaphoreType.DMA((10,)),
            pltpu.SemaphoreType.REGULAR,
        ],
        compiler_params=pltpu.CompilerParams(
            collective_id=0, has_side_effects=True, vmem_limit_bytes=67043328
        ),
    )(
        block_counts,
        jnp.transpose(send_rows[0]),
        source_slots.reshape(16, 128),
        target_slots.reshape(16, 128),
        target_slots,
        return_rows.reshape(32, 128),
        return_rows,
        bond_states,
        angular_basis,
        pre_inner,
        pre_outer,
        jnp.swapaxes(down_proj, 1, 2),
        jnp.swapaxes(bilinear, 1, 2),
        up_proj,
        post_inner,
        post_outer,
    )
    last = pl.BlockSpec((1, 512, 512), lambda g: (1, 0, 0))
    return pl.pallas_call(
        final,
        name="final",
        grid=(4,),
        out_shape=jax.ShapeDtypeStruct((2048, 512), bf16),
        in_specs=[
            pl.BlockSpec((512, 512), lambda g: (g, 0)),
            pl.BlockSpec((512, 256), lambda g: (0, 0)),
            pl.BlockSpec((1, 64, 512), lambda g: (1, 0, 0)),
            last,
            last,
        ],
        out_specs=pl.BlockSpec((512, 512), lambda g: (g, 0)),
    )(inner, message, up_proj, post_inner, post_outer)


def solution(mesh):
    split = ("bond", "atom")
    in_specs = (
        P(split, None),
        P(split),
        P(split, None, None),
        P(split, None),
        P(split, None),
        P(split, None),
        P(split, None, None),
    ) + (P(),) * 7
    return jax.shard_map(
        on_device, mesh=mesh, in_specs=in_specs, out_specs=P(split, None), check_vma=False
    )
```
